32 devices in a mesh: dp: 2 (over y), row: 4 (over z), col: 4 (over x, core).
Axes of the slice: x: 2, y: 2, z: 4, core: 2. Of those that a mesh axis runs over, the one named last changes fastest.
Arguments:
- hidden_in: float32 [2048, 1024], P(('dp', 'col'), 'row'), may hold values from -6 to 6
- segments: int32 [2, 1024], P('dp'), may hold values from 0 to 2, never falling along the last dimension, each value on 1 to 600 neighbouring positions
- norm_in: float32 [1024], P('row'), may hold values from 0.5 to 1.5
- w_query: bfloat16 [1024, 1024], P('row', 'col'), may hold values from -0.1875 to 0.1875
- w_key: bfloat16 [1024, 512], P('row', 'col'), may hold values from -0.1875 to 0.1875
- w_value: bfloat16 [1024, 512], P('row', 'col'), may hold values from -0.1875 to 0.1875
- query_gain: float32 [64], replicated, may hold values from 0.5 to 1.5
- key_gain: float32 [64], replicated, may hold values from 0.5 to 1.5
- w_out: bfloat16 [1024, 1024], P('col', 'row'), may hold values from -0.75 to 0.75
- norm_mid: float32 [1024], P('row'), may hold values from 0.5 to 1.5
- w_gate: bfloat16 [1024, 4608], P('row', 'col'), may hold values from -0.1875 to 0.1875
- w_up: bfloat16 [1024, 4608], P('row', 'col'), may hold values from -0.1875 to 0.1875
- w_down: bfloat16 [4608, 1024], P('col', 'row'), may hold values from -0.15625 to 0.15625
- cotangent: float32 [2048, 1024], P(('dp', 'col'), 'row'), may hold values from -6 to 6
Outputs:
- output: float32 [2048, 1024], P(('dp', 'col'), 'row')
- grad_hidden: float32 [2048, 1024], P(('dp', 'col'), 'row')
- grad_norm_in: float32 [1024], P('row')
- grad_query: float32 [1024, 1024], P('row', 'col')
- grad_key: float32 [1024, 512], P('row', 'col')
- grad_value: float32 [1024, 512], P('row', 'col')
- grad_query_gain: float32 [64], replicated
- grad_key_gain: float32 [64], replicated
- grad_out: float32 [1024, 1024], P('col', 'row')
- grad_norm_mid: float32 [1024], P('row')
- grad_gate: float32 [1024, 4608], P('row', 'col')
- grad_up: float32 [1024, 4608], P('row', 'col')
- grad_down: float32 [4608, 1024], P('col', 'row')
The draws below stay inside these ranges and needn't reach their ends.
Inputs may be any that keep to these rules, and one draw needn't show every extreme that they name: `segments`: within each row the numbers never fall; each of the 3 documents has 1 to 600 tokens, and one has exactly 600.
All inputs are finite; a program needn't handle non-finite values.
Results may differ from the reference program's by a relative error of at most 0.017.
Values may be sent and summed in bfloat16 or wider, within the bound.
A program may use at most 128 MiB of HBM per device.

```python
import math
import jax
import jax.numpy as jnp
import numpy as np
from jax import lax

D = 1024
HEADS = 16
KV_HEADS = 8
HEAD_DIM = 64
FF = 4608
LEN = 1024
SEGS = 3
DOC_MOST = 600
N_SEQ = 2
TOKENS = 2048


def level_of(stream_key, shape, shards, smallest, largest):
    def one(dim, shards_of):
        heights = jax.random.uniform(jax.random.fold_in(jax.random.fold_in(stream_key, 6), dim), (shards_of,), jnp.float32, smallest / len(shards), largest / len(shards))
        return jnp.repeat(jnp.exp(heights), shape[dim] // shards_of).reshape((-1,) + (1,) * (len(shape) - dim - 1))

    factor_of = one(*shards[0])
    for cut in shards[1:]:
        factor_of = factor_of * one(*cut)
    return factor_of


def split_up(count, total, limit, slope):
    portions = [(1 << 20) // math.isqrt(standing ** slope) + 1 for standing in range(2, count + 1)]
    surplus, given = total - limit - (count - 1), [1] * (count - 1)
    while surplus > 0:
        movable = [i for i in range(count - 1) if given[i] < limit]
        whole, left = sum([portions[i] for i in movable]), surplus
        for i in movable:
            extra = min(limit - given[i], max(1, left * portions[i] // whole), surplus)
            given[i] = given[i] + extra
            surplus = surplus - extra
    return np.array([limit] + given)


def ragged(rng, amount, total, bound, skew):
    if amount == 2:
        one = jax.random.randint(rng, (), max(1, total - bound), min(bound, total - 1) + 1)
        return jnp.stack([one, total - one])
    tallies = jnp.asarray(split_up(amount, total, bound, skew), jnp.int32)
    twos = (amount - 1) // 2
    source_of, receiver = tallies[1:1 + 2 * twos:2], tallies[2:2 + 2 * twos:2]
    slack = jnp.minimum(source_of - 1, bound - receiver)
    passed = jax.random.randint(jax.random.fold_in(rng, 1), (twos,), 0, 1 << 20) % (slack + 1)
    tallies = tallies.at[1:1 + 2 * twos:2].set(source_of - passed).at[2:2 + 2 * twos:2].set(receiver + passed)
    return tallies[jax.random.permutation(jax.random.fold_in(rng, 2), amount)]


def scatter_about(rng, dims, scale, most, cuts=(), kind=jnp.bfloat16):
    result = scale * jax.random.normal(rng, dims, jnp.float32)
    if cuts:
        result = result * level_of(rng, dims, cuts, -0.22, 0.18)
    return jnp.clip(result, -most, most).astype(kind)


def setup_inputs(seed: int = 0) -> dict:
    streams_of = jax.random.split(jax.random.key(seed), 15)
    hidden_in = scatter_about(streams_of[0], (TOKENS, D), 1.0, 6.0, ((0, 8), (1, 4)), jnp.float32)
    segments = jax.vmap(lambda own: jnp.searchsorted(jnp.cumsum(ragged(own, SEGS, LEN, DOC_MOST, 1)), jnp.arange(LEN), side="right"))(jax.random.split(streams_of[1], N_SEQ)).reshape((N_SEQ, LEN)).astype(jnp.int32)
    norm_in = jnp.clip(1.0 + 0.1 * jax.random.normal(streams_of[2], (D,), jnp.float32), 0.5, 1.5)
    w_query = scatter_about(streams_of[3], (D, HEADS * HEAD_DIM), D ** -0.5, 0.1875, ((0, 4), (1, 4)))
    w_key = scatter_about(streams_of[4], (D, KV_HEADS * HEAD_DIM), D ** -0.5, 0.1875, ((0, 4), (1, 4)))
    w_value = scatter_about(streams_of[5], (D, KV_HEADS * HEAD_DIM), D ** -0.5, 0.1875, ((0, 4), (1, 4)))
    query_gain = jnp.clip(1.0 + 0.1 * jax.random.normal(streams_of[6], (HEAD_DIM,), jnp.float32), 0.5, 1.5)
    key_gain = jnp.clip(1.0 + 0.1 * jax.random.normal(streams_of[7], (HEAD_DIM,), jnp.float32), 0.5, 1.5)
    w_out = scatter_about(streams_of[8], (HEADS * HEAD_DIM, D), (HEADS * HEAD_DIM // 16) ** -0.5, 0.75, ((0, 4), (1, 4)))
    norm_mid = jnp.clip(1.0 + 0.1 * jax.random.normal(streams_of[9], (D,), jnp.float32), 0.5, 1.5)
    w_gate = scatter_about(streams_of[10], (D, FF), D ** -0.5, 0.1875, ((0, 4), (1, 4)))
    w_up = scatter_about(streams_of[11], (D, FF), D ** -0.5, 0.1875, ((0, 4), (1, 4)))
    w_down = scatter_about(streams_of[12], (FF, D), (FF // 3) ** -0.5, 0.15625, ((0, 4), (1, 4)))
    cotangent = scatter_about(streams_of[13], (TOKENS, D), 1.0, 6.0, ((0, 8), (1, 4)), jnp.float32)
    return dict(hidden_in=hidden_in, segments=segments, norm_in=norm_in, w_query=w_query, w_key=w_key, w_value=w_value, query_gain=query_gain, key_gain=key_gain, w_out=w_out, norm_mid=norm_mid, w_gate=w_gate, w_up=w_up, w_down=w_down, cotangent=cotangent)


epsilon = 1e-05
rope_base = 1000000.0

def positions_of(documents):
    length = documents.shape[0]
    places = jnp.arange(length, dtype=jnp.int32)
    starts_here = jnp.concatenate([places[:1] >= 0, documents[1:] != documents[:-1]])
    doc_start = lax.cummax(jnp.where(starts_here, places, 0).astype(jnp.int32), axis=0)
    return places - doc_start

def rotary_tables(positions):
    half_dim = HEAD_DIM // 2
    frequency = rope_base ** (-2.0 * jnp.arange(half_dim, dtype=jnp.float32) / HEAD_DIM)
    angles = positions.astype(jnp.float32)[:, None] * frequency[None, :]
    return (jnp.cos(angles)[:, None, :], jnp.sin(angles)[:, None, :])

def rotate(values, cos_table, sin_table):
    half_dim = HEAD_DIM // 2
    first_half, second = (values[..., :half_dim], values[..., half_dim:])
    return jnp.concatenate([first_half * cos_table - second * sin_table, second * cos_table + first_half * sin_table], axis=-1)

def rotate_back(gradient, cos_table, sin_table):
    half_dim = HEAD_DIM // 2
    first_half, second = (gradient[..., :half_dim], gradient[..., half_dim:])
    return jnp.concatenate([first_half * cos_table + second * sin_table, second * cos_table - first_half * sin_table], axis=-1)

def head_rates(values):
    return lax.rsqrt(lax.optimization_barrier(jnp.mean(values * values, axis=-1, keepdims=True)) + epsilon)

def head_back(values, rate_rows, gain, gradient):
    scaled = gain * gradient
    inner_mean = lax.optimization_barrier(jnp.mean(scaled * values, axis=-1, keepdims=True))
    return (rate_rows * scaled - values * rate_rows ** 3 * inner_mean, lax.optimization_barrier(jnp.sum(gradient * values * rate_rows, axis=(0, 1))))

def one_sequence(hidden, cotan, documents, weights):
    norm_in, w_query, w_key, w_value, query_gain, key_gain, w_out, norm_mid, w_gate, w_up, w_down = weights
    length = hidden.shape[0]
    q_cols = HEADS * HEAD_DIM
    k_cols = KV_HEADS * HEAD_DIM
    groups = HEADS // KV_HEADS
    scale_factor = HEAD_DIM ** (-0.5)
    flt = jnp.float32
    low = jnp.bfloat16
    rate_in = lax.rsqrt(lax.optimization_barrier(jnp.mean(hidden * hidden, axis=1, keepdims=True)) + epsilon)
    normed_in = (hidden * rate_in * norm_in).astype(low)
    w_joined = jnp.concatenate([w_query, w_key, w_value], axis=1)
    projected = jnp.dot(normed_in, w_joined, preferred_element_type=flt)
    raw_query = projected[:, :q_cols].reshape(length, HEADS, HEAD_DIM)
    raw_key = projected[:, q_cols:q_cols + k_cols].reshape(length, KV_HEADS, HEAD_DIM)
    value_low = projected[:, q_cols + k_cols:].astype(low)
    cos_table, sin_table = rotary_tables(positions_of(documents))
    query_rate = head_rates(raw_query)
    key_rate = head_rates(raw_key)
    query_rot = rotate(raw_query * query_rate * query_gain, cos_table, sin_table).astype(low)
    key_rot = rotate(raw_key * key_rate * key_gain, cos_table, sin_table).astype(low)
    places = jnp.arange(length, dtype=jnp.int32)
    allowed = (documents[:, None] == documents[None, :]) & (places[:, None] >= places[None, :])
    query_blocks = query_rot.reshape(length, KV_HEADS, groups, HEAD_DIM).astype(flt)
    key_heads = key_rot.astype(flt)
    value_heads = value_low.reshape(length, KV_HEADS, HEAD_DIM).astype(flt)
    scores = jnp.einsum('qkgd,skd->kgqs', query_blocks, key_heads) * scale_factor
    log_total = jnp.log(lax.optimization_barrier(jnp.sum(jnp.where(allowed, jnp.exp(scores), 0.0), axis=-1, keepdims=True)))
    probability = jnp.where(allowed, jnp.exp(scores - log_total), 0.0)
    prob_low = probability.astype(low).astype(flt)
    mixed = jnp.einsum('kgqs,skd->qkgd', prob_low, value_heads).reshape(length, q_cols).astype(low)
    resid = hidden + jnp.dot(mixed, w_out, preferred_element_type=flt)
    rate_mid = lax.rsqrt(lax.optimization_barrier(jnp.mean(resid * resid, axis=1, keepdims=True)) + epsilon)
    normed_mid = (resid * rate_mid * norm_mid).astype(low)
    gate_pre = jnp.dot(normed_mid, w_gate, preferred_element_type=flt)
    up_pre = jnp.dot(normed_mid, w_up, preferred_element_type=flt)
    sigmoid_gate = jax.nn.sigmoid(gate_pre)
    activated = gate_pre * sigmoid_gate
    swiglu = (activated * up_pre).astype(low)
    output = resid + jnp.dot(swiglu, w_down, preferred_element_type=flt)
    cot_low = cotan.astype(low)
    grad_down = jnp.dot(swiglu.T, cot_low, preferred_element_type=flt)
    grad_swiglu = jnp.dot(cot_low, w_down.T, preferred_element_type=flt)
    grad_gate_act = (grad_swiglu * up_pre * sigmoid_gate * (1.0 + gate_pre * (1.0 - sigmoid_gate))).astype(low)
    grad_up_act = (grad_swiglu * activated).astype(low)
    grad_gate = jnp.dot(normed_mid.T, grad_gate_act, preferred_element_type=flt)
    grad_up = jnp.dot(normed_mid.T, grad_up_act, preferred_element_type=flt)
    grad_normed_mid = jnp.dot(grad_gate_act, w_gate.T, preferred_element_type=flt) + jnp.dot(grad_up_act, w_up.T, preferred_element_type=flt)
    scaled_mid = norm_mid * grad_normed_mid
    grad_resid = cotan + rate_mid * scaled_mid - resid * rate_mid ** 3 * lax.optimization_barrier(jnp.mean(scaled_mid * resid, axis=1, keepdims=True))
    grad_norm_mid = lax.optimization_barrier(jnp.sum(grad_normed_mid * resid * rate_mid, axis=0))
    resid_low = grad_resid.astype(low)
    grad_out = jnp.dot(mixed.T, resid_low, preferred_element_type=flt)
    grad_mixed = jnp.dot(resid_low, w_out.T, preferred_element_type=flt).astype(low)
    grad_mixed_heads = grad_mixed.reshape(length, KV_HEADS, groups, HEAD_DIM).astype(flt)
    grad_value_act = jnp.einsum('kgqs,qkgd->skd', prob_low, grad_mixed_heads)
    grad_probs = jnp.einsum('qkgd,skd->kgqs', grad_mixed_heads, value_heads)
    row_inner = lax.optimization_barrier(jnp.sum(probability * grad_probs, axis=-1, keepdims=True))
    grad_scores = (probability * (grad_probs - row_inner) * scale_factor).astype(low).astype(flt)
    grad_query_rot = jnp.einsum('kgqs,skd->qkgd', grad_scores, key_heads).reshape(length, HEADS, HEAD_DIM)
    grad_key_rot = jnp.einsum('kgqs,qkgd->skd', grad_scores, query_blocks)
    grad_raw_query, grad_query_gain = head_back(raw_query, query_rate, query_gain, rotate_back(grad_query_rot, cos_table, sin_table))
    grad_raw_key, grad_key_gain = head_back(raw_key, key_rate, key_gain, rotate_back(grad_key_rot, cos_table, sin_table))
    grad_proj = jnp.concatenate([grad_raw_query.reshape(length, q_cols), grad_raw_key.reshape(length, k_cols), grad_value_act.reshape(length, k_cols)], axis=1).astype(low)
    grad_joined = jnp.dot(normed_in.T, grad_proj, preferred_element_type=flt)
    grad_normed_in = jnp.dot(grad_proj, w_joined.T, preferred_element_type=flt)
    scaled_in = norm_in * grad_normed_in
    grad_hidden = grad_resid + rate_in * scaled_in - hidden * rate_in ** 3 * lax.optimization_barrier(jnp.mean(scaled_in * hidden, axis=1, keepdims=True))
    grad_norm_in = lax.optimization_barrier(jnp.sum(grad_normed_in * hidden * rate_in, axis=0))
    gradients = (grad_norm_in, grad_joined[:, :q_cols], grad_joined[:, q_cols:q_cols + k_cols], grad_joined[:, q_cols + k_cols:], grad_query_gain, grad_key_gain, grad_out, grad_norm_mid, grad_gate, grad_up, grad_down)
    return (output, grad_hidden, gradients)

def reference(hidden_in, segments, norm_in, w_query, w_key, w_value, query_gain, key_gain, w_out, norm_mid, w_gate, w_up, w_down, cotangent):
    weights = (norm_in, w_query, w_key, w_value, query_gain, key_gain, w_out, norm_mid, w_gate, w_up, w_down)
    totals = tuple((jnp.zeros(weight.shape, jnp.float32) for weight in weights))
    stacked = (hidden_in.reshape(N_SEQ, LEN, D), cotangent.reshape(N_SEQ, LEN, D), segments)

    def advance(carried, item):
        hidden, cotan, documents = item
        output, grad_hidden, gradients = one_sequence(hidden, cotan, documents, weights)
        return (jax.tree.map(lambda left_side, right_side: left_side + right_side, carried, gradients), (output, grad_hidden))
    totals, (outputs, grad_rows) = lax.scan(advance, totals, stacked)
    return (outputs.reshape(TOKENS, D), grad_rows.reshape(TOKENS, D), totals[0], totals[1], totals[2], totals[3], totals[4], totals[5], totals[6], totals[7], totals[8], totals[9], totals[10])
```

```python
import functools

import jax
import jax.numpy as jnp
from jax import lax
from jax.experimental import pallas as pl
from jax.experimental.pallas import tpu as pltpu
from jax.sharding import PartitionSpec as P

HEAD_DIM = 64


epsilon = 1e-05
rope_base = 1000000.0


def positions_of(documents):
    length = documents.shape[0]
    places = jnp.arange(length, dtype=jnp.int32)
    starts_here = jnp.concatenate([places[:1] >= 0, documents[1:] != documents[:-1]])
    doc_start = lax.cummax(jnp.where(starts_here, places, 0), axis=0)
    return places - doc_start


def rotary_tables(positions):
    half_dim = HEAD_DIM // 2
    frequency = rope_base ** (-2.0 * jnp.arange(half_dim, dtype=jnp.float32) / HEAD_DIM)
    angles = positions.astype(jnp.float32)[:, None] * frequency[None, :]
    return (jnp.cos(angles)[:, None, :], jnp.sin(angles)[:, None, :])


def rotate(values, cos_table, sin_table):
    half_dim = HEAD_DIM // 2
    first_half, second = (values[..., :half_dim], values[..., half_dim:])
    return jnp.concatenate(
        [first_half * cos_table - second * sin_table, second * cos_table + first_half * sin_table],
        axis=-1,
    )


def rotate_back(gradient, cos_table, sin_table):
    half_dim = HEAD_DIM // 2
    first_half, second = (gradient[..., :half_dim], gradient[..., half_dim:])
    return jnp.concatenate(
        [first_half * cos_table + second * sin_table, second * cos_table - first_half * sin_table],
        axis=-1,
    )


def head_rates(values):
    return lax.rsqrt(jnp.mean(values * values, axis=-1, keepdims=True) + epsilon)


def head_back(values, rate_rows, gain, gradient):
    scaled = gain * gradient
    inner_mean = jnp.mean(scaled * values, axis=-1, keepdims=True)
    return (
        rate_rows * scaled - values * rate_rows**3 * inner_mean,
        jnp.sum(gradient * values * rate_rows, axis=(0, 1)),
    )


def part(ref, dim, index, size):
    if dim is None:
        return ref
    if dim == "lead":
        return ref.at[index]
    start = pl.multiple_of(index * size, size)
    return ref.at[(slice(None),) * dim + (pl.ds(start, size),)]


def swap_kernel(ops, sizes, *refs):
    count = len(ops)
    ins, outs = refs[:count], refs[count : 2 * count]
    send_sem, recv_sem, own_sem = refs[2 * count :]
    axes = sorted({op[0] for op in ops})
    me = {axis: lax.axis_index(axis) for axis in axes}
    barrier = pltpu.get_barrier_semaphore()
    for axis in axes:
        for step in range(1, sizes[axis]):
            pl.semaphore_signal(
                barrier,
                inc=1,
                device_id={axis: lax.rem(me[axis] + step, sizes[axis])},
                device_id_type=pl.DeviceIdType.MESH,
            )
    pl.semaphore_wait(barrier, sum(sizes[axis] - 1 for axis in axes))
    copies = []
    slot = 0
    for place, (axis, src_dim, src_size, dst_dim, dst_size) in enumerate(ops):
        for step in range(1, sizes[axis]):
            peer = lax.rem(me[axis] + step, sizes[axis])
            copy = pltpu.make_async_remote_copy(
                src_ref=part(ins[place], src_dim, peer, src_size),
                dst_ref=part(outs[place], dst_dim, me[axis], dst_size),
                send_sem=send_sem.at[slot],
                recv_sem=recv_sem.at[slot],
                device_id={axis: peer},
                device_id_type=pl.DeviceIdType.MESH,
            )
            copy.start()
            copies.append(copy)
            slot += 1
    for place, (axis, src_dim, src_size, dst_dim, dst_size) in enumerate(ops):
        copy = pltpu.make_async_copy(
            part(ins[place], src_dim, me[axis], src_size),
            part(outs[place], dst_dim, me[axis], dst_size),
            own_sem.at[place],
        )
        copy.start()
        copies.append(copy)
    for copy in copies:
        copy.wait()


def swap(ident, *ops):
    sizes = {op[0]: lax.axis_size(op[0]) for op in ops}
    plans, shapes = [], []
    for axis, array, src_dim, dst_dim in ops:
        n = sizes[axis]
        block = list(array.shape)
        src_size = dst_size = None
        if src_dim == "lead":
            block = block[1:]
        elif src_dim is not None:
            block[src_dim] //= n
            src_size = block[src_dim]
        if dst_dim == "lead":
            block = [n] + block
        else:
            dst_size = block[dst_dim]
            block[dst_dim] *= n
        plans.append((axis, src_dim, src_size, dst_dim, dst_size))
        shapes.append(jax.ShapeDtypeStruct(tuple(block), array.dtype))
    slots = sum(sizes[op[0]] - 1 for op in ops)
    return pl.pallas_call(
        functools.partial(swap_kernel, tuple(plans), sizes),
        out_shape=tuple(shapes),
        in_specs=[pl.BlockSpec(memory_space=pltpu.VMEM)] * len(ops),
        out_specs=(pl.BlockSpec(memory_space=pltpu.VMEM),) * len(ops),
        scratch_shapes=[
            pltpu.SemaphoreType.DMA((slots,)),
            pltpu.SemaphoreType.DMA((slots,)),
            pltpu.SemaphoreType.DMA((len(ops),)),
        ],
        compiler_params=pltpu.CompilerParams(collective_id=ident, has_side_effects=True),
    )(*[op[1] for op in ops])


def dot(left_side, right_side):
    return jnp.dot(left_side, right_side, preferred_element_type=jnp.float32)


def dot_turned(left_side, right_side):
    return lax.dot_general(
        left_side, right_side, (((1,), (1,)), ((), ())), preferred_element_type=jnp.float32
    )


def outer_sum(left_side, right_side):
    return lax.dot_general(
        left_side, right_side, (((0,), (0,)), ((), ())), preferred_element_type=jnp.float32
    )


def eight(vector):
    return jnp.broadcast_to(vector[None, :], (8,) + vector.shape)


def added(stacked):
    return jnp.sum(stacked.astype(jnp.float32), axis=0)


def local(
    hidden_in,
    segments,
    norm_in,
    w_query,
    w_key,
    w_value,
    query_gain,
    key_gain,
    w_out,
    norm_mid,
    w_gate,
    w_up,
    w_down,
    cotangent,
):
    low = jnp.bfloat16
    flt = jnp.float32
    rows = lax.axis_size("row")
    slab_rows, feature_slab = hidden_in.shape
    model_width = feature_slab * rows
    q_cols = w_query.shape[1]
    k_cols = w_key.shape[1]
    q_mine = q_cols // HEAD_DIM // rows
    kv_local = k_cols // HEAD_DIM
    kv_mine = max(1, kv_local // rows)
    share = rows * kv_mine // kv_local
    groups = q_mine // kv_mine
    q_width, k_width = q_mine * HEAD_DIM, kv_mine * HEAD_DIM
    ff_local = w_gate.shape[1]
    ff_mine = ff_local // rows
    scale_factor = HEAD_DIM ** (-0.5)
    seq_local, length = segments.shape
    stream = seq_local * length
    documents = (segments + length * jnp.arange(seq_local, dtype=jnp.int32)[:, None]).reshape(
        stream
    )
    places = jnp.arange(stream, dtype=jnp.int32)
    allowed = (documents[:, None] == documents[None, :]) & (places[:, None] >= places[None, :])
    cos_table, sin_table = rotary_tables(positions_of(documents))

    cot_low = cotangent.astype(low)
    cot_all = lax.all_gather(
        lax.all_gather(cot_low, "row", axis=1, tiled=True), "col", axis=0, tiled=True
    )

    w_joined_parts = jnp.stack(
        [
            jnp.concatenate(
                [
                    w_query[:, r * q_width : (r + 1) * q_width],
                    w_key[:, (r // share) * k_width : (r // share + 1) * k_width],
                    w_value[:, (r // share) * k_width : (r // share + 1) * k_width],
                ],
                axis=1,
            )
            for r in range(rows)
        ]
    )
    w_pair_parts = jnp.stack(
        [
            jnp.stack([w[:, r * ff_mine : (r + 1) * ff_mine] for w in (w_gate, w_up)])
            for r in range(rows)
        ]
    )
    hidden_row, square_in, norm_in_all, norm_mid_all, w_joined, w_out_mine = swap(
        0,
        ("row", hidden_in.astype(low), None, 1),
        ("row", eight(jnp.sum(hidden_in * hidden_in, axis=1)), None, "lead"),
        ("row", eight(norm_in), None, 1),
        ("row", eight(norm_mid), None, 1),
        ("row", w_joined_parts, "lead", 0),
        ("row", w_out, 0, 1),
    )
    rate_in = lax.rsqrt(jnp.sum(square_in, axis=0)[0] / model_width + epsilon)[:, None]
    normed_in, w_pair = swap(
        1,
        ("col", (hidden_row.astype(flt) * rate_in * norm_in_all[:1]).astype(low), None, 0),
        ("row", w_pair_parts, "lead", 1),
    )
    projected = dot(normed_in, w_joined)
    raw_query = projected[:, :q_width].reshape(stream, q_mine, HEAD_DIM)
    raw_key = projected[:, q_width : q_width + k_width].reshape(stream, kv_mine, HEAD_DIM)
    value_heads = projected[:, q_width + k_width :].astype(low).reshape(stream, kv_mine, HEAD_DIM)
    query_rate = head_rates(raw_query)
    key_rate = head_rates(raw_key)
    query_rot = rotate(raw_query * query_rate * query_gain, cos_table, sin_table).astype(low)
    key_heads = rotate(raw_key * key_rate * key_gain, cos_table, sin_table).astype(low)
    query_blocks = query_rot.reshape(stream, kv_mine, groups, HEAD_DIM)
    scores = (
        jnp.einsum("qkgd,skd->kgqs", query_blocks, key_heads, preferred_element_type=flt)
        * scale_factor
    )
    log_total = jnp.log(jnp.sum(jnp.where(allowed, jnp.exp(scores), 0.0), axis=-1, keepdims=True))
    probability = jnp.where(allowed, jnp.exp(scores - log_total), 0.0)
    mixed = (
        jnp.einsum(
            "kgqs,skd->qkgd", probability.astype(low), value_heads, preferred_element_type=flt
        )
        .reshape(stream, q_width)
        .astype(low)
    )
    out_parts, w_down_mine = swap(
        2,
        ("col", dot(mixed, w_out_mine).astype(low), 0, "lead"),
        ("row", w_down, 0, 1),
    )
    (out_cols,) = swap(3, ("row", added(out_parts).astype(low), 1, "lead"))
    resid = hidden_in + added(out_cols)
    resid_row, square_mid = swap(
        4,
        ("row", resid.astype(low), None, 1),
        ("row", eight(jnp.sum(resid * resid, axis=1)), None, "lead"),
    )
    rate_mid = lax.rsqrt(jnp.sum(square_mid, axis=0)[0] / model_width + epsilon)[:, None]
    (normed_mid,) = swap(
        5, ("col", (resid_row.astype(flt) * rate_mid * norm_mid_all[:1]).astype(low), None, 0)
    )
    gate_pre = dot(normed_mid, w_pair[0])
    up_pre = dot(normed_mid, w_pair[1])
    sigmoid_gate = jax.nn.sigmoid(gate_pre)
    activated = gate_pre * sigmoid_gate
    swiglu = (activated * up_pre).astype(low)
    down_part = dot(swiglu, w_down_mine).astype(low)
    down_own = lax.psum_scatter(
        lax.psum_scatter(down_part, "col", scatter_dimension=0, tiled=True),
        "row",
        scatter_dimension=1,
        tiled=True,
    )
    output = resid + down_own.astype(flt)
    grad_swiglu = dot_turned(cot_all, w_down_mine)
    grad_down = outer_sum(swiglu, cot_all).astype(low)
    grad_gate_act = (
        grad_swiglu * up_pre * sigmoid_gate * (1.0 + gate_pre * (1.0 - sigmoid_gate))
    ).astype(low)
    grad_up_act = (grad_swiglu * activated).astype(low)
    mid_part = dot_turned(grad_gate_act, w_pair[0]) + dot_turned(grad_up_act, w_pair[1])
    grad_gate = outer_sum(normed_mid, grad_gate_act).astype(low)
    grad_up = outer_sum(normed_mid, grad_up_act).astype(low)
    mid_parts, grad_gate_got, grad_up_got = swap(
        6,
        ("col", mid_part.astype(low), 0, "lead"),
        ("row", grad_gate, 0, "lead"),
        ("row", grad_up, 0, "lead"),
    )
    (mid_cols,) = swap(7, ("row", added(mid_parts).astype(low), 1, "lead"))
    grad_normed_mid = added(mid_cols)
    scaled_mid = norm_mid * grad_normed_mid
    first_mid = cotangent + rate_mid * scaled_mid
    first_row, inner_got = swap(
        8,
        ("row", first_mid.astype(low), None, 1),
        ("row", eight(jnp.sum(scaled_mid * resid, axis=1)), None, "lead"),
    )
    mid_scale = rate_mid**3 * (jnp.sum(inner_got, axis=0)[0][:, None] / model_width)
    grad_resid = first_mid - resid * mid_scale
    gain_mid = jnp.sum(grad_normed_mid * resid * rate_mid, axis=0)
    resid_low, grad_down_got = swap(
        9,
        ("col", (first_row.astype(flt) - resid_row.astype(flt) * mid_scale).astype(low), None, 0),
        ("row", grad_down, 1, 0),
    )

    def unfold(got):
        return jnp.moveaxis(got, 0, 1).reshape(got.shape[1], -1)

    grad_gate, grad_up, grad_down = (
        value.astype(flt)
        for value in lax.psum((unfold(grad_gate_got), unfold(grad_up_got), grad_down_got), "dp")
    )
    grad_out = outer_sum(mixed, resid_low).astype(low)
    grad_mixed_heads = (
        dot_turned(resid_low, w_out_mine).astype(low).reshape(stream, kv_mine, groups, HEAD_DIM)
    )
    grad_value_act = jnp.einsum(
        "kgqs,qkgd->skd", probability.astype(low), grad_mixed_heads, preferred_element_type=flt
    )
    grad_probs = jnp.einsum(
        "qkgd,skd->kgqs", grad_mixed_heads, value_heads, preferred_element_type=flt
    )
    row_inner = jnp.sum(probability * grad_probs, axis=-1, keepdims=True)
    grad_scores = (probability * (grad_probs - row_inner) * scale_factor).astype(low)
    grad_query_rot = jnp.einsum(
        "kgqs,skd->qkgd", grad_scores, key_heads, preferred_element_type=flt
    ).reshape(stream, q_mine, HEAD_DIM)
    grad_key_rot = jnp.einsum(
        "kgqs,qkgd->skd", grad_scores, query_blocks, preferred_element_type=flt
    )
    grad_raw_query, gain_query = head_back(
        raw_query, query_rate, query_gain, rotate_back(grad_query_rot, cos_table, sin_table)
    )
    grad_raw_key, gain_key = head_back(
        raw_key, key_rate, key_gain, rotate_back(grad_key_rot, cos_table, sin_table)
    )
    grad_proj = jnp.concatenate(
        [
            grad_raw_query.reshape(stream, q_width),
            grad_raw_key.reshape(stream, k_width),
            grad_value_act.reshape(stream, k_width),
        ],
        axis=1,
    ).astype(low)
    grad_joined = outer_sum(normed_in, grad_proj).astype(low)
    in_parts, joined_got, out_got = swap(
        10,
        ("col", dot_turned(grad_proj, w_joined).astype(low), 0, "lead"),
        ("row", grad_joined, 0, "lead"),
        ("row", grad_out, 1, 0),
    )
    (in_cols,) = swap(11, ("row", added(in_parts).astype(low), 1, "lead"))
    grad_normed_in = added(in_cols)
    scaled_in = norm_in * grad_normed_in
    (in_inner,) = swap(12, ("row", eight(jnp.sum(scaled_in * hidden_in, axis=1)), None, "lead"))
    in_scale = rate_in**3 * (jnp.sum(in_inner, axis=0)[0][:, None] / model_width)
    grad_hidden = grad_resid + rate_in * scaled_in - hidden_in * in_scale
    gain_in = jnp.sum(grad_normed_in * hidden_in * rate_in, axis=0)

    def shared(got):
        summed = got.astype(flt).reshape(rows // share, share, feature_slab, k_width).sum(axis=1)
        return unfold(summed).astype(low)

    grad_query, grad_key, grad_value, grad_out = (
        value.astype(flt)
        for value in lax.psum(
            (
                unfold(joined_got[:, :, :q_width]),
                shared(joined_got[:, :, q_width : q_width + k_width]),
                shared(joined_got[:, :, q_width + k_width :]),
                out_got,
            ),
            "dp",
        )
    )
    block_start = lax.axis_index("row") * feature_slab
    spread_in = lax.dynamic_update_slice(jnp.zeros((model_width,), flt), gain_in, (block_start,))
    spread_mid = lax.dynamic_update_slice(jnp.zeros((model_width,), flt), gain_mid, (block_start,))
    sum_in, sum_mid, gain_query, gain_key = lax.psum(
        (spread_in, spread_mid, gain_query, gain_key), ("dp", "row", "col")
    )
    gain_in = lax.dynamic_slice(sum_in, (block_start,), (feature_slab,))
    gain_mid = lax.dynamic_slice(sum_mid, (block_start,), (feature_slab,))
    return (
        output,
        grad_hidden,
        gain_in,
        grad_query,
        grad_key,
        grad_value,
        gain_query,
        gain_key,
        grad_out,
        gain_mid,
        grad_gate,
        grad_up,
        grad_down,
    )


def solution(mesh):
    return jax.shard_map(
        local,
        mesh=mesh,
        in_specs=(
            P(("dp", "col"), "row"),
            P("dp", None),
            P("row"),
            P("row", "col"),
            P("row", "col"),
            P("row", "col"),
            P(),
            P(),
            P("col", "row"),
            P("row"),
            P("row", "col"),
            P("row", "col"),
            P("col", "row"),
            P(("dp", "col"), "row"),
        ),
        out_specs=(
            P(("dp", "col"), "row"),
            P(("dp", "col"), "row"),
            P("row"),
            P("row", "col"),
            P("row", "col"),
            P("row", "col"),
            P(),
            P(),
            P("col", "row"),
            P("row"),
            P("row", "col"),
            P("row", "col"),
            P("col", "row"),
        ),
        check_vma=False,
    )
```

```python
import functools

import jax
import jax.numpy as jnp
from jax import lax
from jax.experimental import pallas as pl
from jax.experimental.pallas import tpu as pltpu
from jax.sharding import PartitionSpec as P

HEAD_DIM = 64


epsilon = 1e-05
rope_base = 1000000.0


def positions_of(documents):
    length = documents.shape[0]
    places = jnp.arange(length, dtype=jnp.int32)
    starts_here = jnp.concatenate([places[:1] >= 0, documents[1:] != documents[:-1]])
    doc_start = lax.cummax(jnp.where(starts_here, places, 0), axis=0)
    return places - doc_start


def rotary_tables(positions):
    half_dim = HEAD_DIM // 2
    frequency = rope_base ** (-2.0 * jnp.arange(half_dim, dtype=jnp.float32) / HEAD_DIM)
    angles = positions.astype(jnp.float32)[:, None] * frequency[None, :]
    return (jnp.cos(angles)[:, None, :], jnp.sin(angles)[:, None, :])


def rotate(values, cos_table, sin_table):
    half_dim = HEAD_DIM // 2
    first_half, second = (values[..., :half_dim], values[..., half_dim:])
    return jnp.concatenate(
        [first_half * cos_table - second * sin_table, second * cos_table + first_half * sin_table],
        axis=-1,
    )


def rotate_back(gradient, cos_table, sin_table):
    half_dim = HEAD_DIM // 2
    first_half, second = (gradient[..., :half_dim], gradient[..., half_dim:])
    return jnp.concatenate(
        [first_half * cos_table + second * sin_table, second * cos_table - first_half * sin_table],
        axis=-1,
    )


def head_rates(values):
    return lax.rsqrt(jnp.mean(values * values, axis=-1, keepdims=True) + epsilon)


def head_back(values, rate_rows, gain, gradient):
    scaled = gain * gradient
    inner_mean = jnp.mean(scaled * values, axis=-1, keepdims=True)
    return (
        rate_rows * scaled - values * rate_rows**3 * inner_mean,
        jnp.sum(gradient * values * rate_rows, axis=(0, 1)),
    )


def part(ref, dim, index, size):
    if dim is None:
        return ref
    if dim == "lead":
        return ref.at[index]
    start = pl.multiple_of(index * size, size)
    return ref.at[(slice(None),) * dim + (pl.ds(start, size),)]


def send_to(src, dst, sends, recvs, slot, axis, peer):
    copy = pltpu.make_async_remote_copy(
        src_ref=src,
        dst_ref=dst,
        send_sem=sends.at[slot],
        recv_sem=recvs.at[slot],
        device_id={axis: peer},
        device_id_type=pl.DeviceIdType.MESH,
    )
    copy.start()
    return copy


def push_steps(plan, n, me, ins, outs, scratch):
    axis, src_dim, src_size, dst_dim, dst_size = plan
    sends, recvs, own = scratch
    copies = []
    for step in range(1, n):
        peer = lax.rem(me + step, n)
        copies.append(
            send_to(
                part(ins[0], src_dim, peer, src_size),
                part(outs[0], dst_dim, me, dst_size),
                sends,
                recvs,
                step - 1,
                axis,
                peer,
            )
        )
    copy = pltpu.make_async_copy(
        part(ins[0], src_dim, me, src_size), part(outs[0], dst_dim, me, dst_size), own.at[0]
    )
    copy.start()
    copies.append(copy)
    yield
    yield
    yield
    for copy in copies:
        copy.wait()


def partners(me):
    near = me + 1 - 2 * lax.rem(me, 2)
    far = lax.rem(me + 2, 4)
    return near, far, lax.rem(near + 2, 4)


def span(block, rows, piece, pieces):
    size = rows // pieces
    return pl.ds(pl.multiple_of(block * rows + piece * size, size), size)


def relay_gather_steps(plan, n, me, ins, outs, scratch):
    axis, pieces = plan
    sends, recvs, own = scratch
    rows = ins[0].shape[0]
    near, far, _ = partners(me)
    size = rows // pieces
    firsts = [
        send_to(
            ins[0].at[pl.ds(p * size, size)],
            outs[0].at[span(me, rows, p, pieces)],
            sends,
            recvs,
            p,
            axis,
            far,
        )
        for p in range(pieces)
    ]
    beside = send_to(
        ins[0], outs[0].at[span(me, rows, 0, 1)], sends, recvs, pieces, axis, near
    )
    mine = pltpu.make_async_copy(ins[0], outs[0].at[span(me, rows, 0, 1)], own.at[0])
    mine.start()
    yield
    relays = []
    for p in range(pieces):
        firsts[p].wait_recv()
        place = span(far, rows, p, pieces)
        relays.append(
            send_to(
                outs[0].at[place], outs[0].at[place], sends, recvs, pieces + 1 + p, axis, near
            )
        )
    yield
    for copy in firsts:
        copy.wait_send()
    beside.wait()
    for copy in relays:
        copy.wait()
    mine.wait()


def relay_reduce_steps(plan, n, me, ins, outs, scratch):
    axis, pieces = plan
    sends, recvs, from_near, passed, from_far = scratch
    flt = jnp.float32
    rows = outs[0].shape[0]
    size = rows // pieces
    near, far, across = partners(me)
    firsts = [
        send_to(
            ins[0].at[span(across, rows, p, pieces)],
            from_near.at[pl.ds(p * size, size)],
            sends,
            recvs,
            p,
            axis,
            near,
        )
        for p in range(pieces)
    ]
    beside = send_to(
        ins[0].at[span(near, rows, 0, 1)],
        from_near.at[pl.ds(rows, rows)],
        sends,
        recvs,
        pieces,
        axis,
        near,
    )
    yield
    seconds = []
    for p in range(pieces):
        here = pl.ds(p * size, size)
        firsts[p].wait_recv()
        passed[here, :] = (
            ins[0][span(far, rows, p, pieces), :].astype(flt) + from_near[here, :].astype(flt)
        ).astype(passed.dtype)
        seconds.append(
            send_to(
                passed.at[here], from_far.at[here], sends, recvs, pieces + 1 + p, axis, far
            )
        )
    beside.wait_recv()
    yield
    for p in range(pieces):
        here = pl.ds(p * size, size)
        seconds[p].wait_recv()
        outs[0][here, :] = (
            ins[0][span(me, rows, p, pieces), :].astype(flt)
            + from_near[pl.ds(rows + p * size, size), :].astype(flt)
            + from_far[here, :].astype(flt)
        ).astype(outs[0].dtype)
    for copy in firsts + [beside] + seconds:
        copy.wait_send()


def reduce_gather_steps(plan, n, me, ins, outs, scratch):
    axis, pieces, added_to, gained = plan
    sends, recvs, got, mine = scratch
    flt = jnp.float32
    rows, width = outs[0].shape
    size = rows // pieces
    own_columns = pl.ds(pl.multiple_of(me * width, width), width)
    arriving = []
    for p in range(pieces):
        here = pl.ds(p * size, size)
        arriving.append(
            [
                send_to(
                    ins[0].at[
                        here,
                        pl.ds(pl.multiple_of(lax.rem(me + step, n) * width, width), width),
                    ],
                    got.at[step - 1, here],
                    sends,
                    recvs,
                    p * (n - 1) + step - 1,
                    axis,
                    lax.rem(me + step, n),
                )
                for step in range(1, n)
            ]
        )
    yield
    leaving = []
    for p in range(pieces):
        here = pl.ds(p * size, size)
        total = ins[0][here, own_columns].astype(flt)
        for step in range(1, n):
            arriving[p][step - 1].wait_recv()
            total = total + got[step - 1, here].astype(flt)
        if added_to:
            total = total + ins[1][here, :]
        outs[0][here, :] = total
        if gained:
            total = total * ins[1][0:1, :]
        mine[here, :] = total.astype(mine.dtype)
        outs[1][here, own_columns] = total.astype(mine.dtype)
        for step in range(1, n):
            leaving.append(
                send_to(
                    mine.at[here],
                    outs[1].at[here, own_columns],
                    sends,
                    recvs,
                    (pieces + p) * (n - 1) + step - 1,
                    axis,
                    lax.rem(me + step, n),
                )
            )
    yield
    for copies in arriving:
        for copy in copies:
            copy.wait_send()
    for copy in leaving:
        copy.wait()


STEPS = {
    "push": push_steps,
    "relay_gather": relay_gather_steps,
    "relay_reduce": relay_reduce_steps,
    "reduce_gather": reduce_gather_steps,
}


def exchange_kernel(jobs, sizes, *refs):
    me = {axis: lax.axis_index(axis) for axis in sizes}
    barrier = pltpu.get_barrier_semaphore()
    for axis in sizes:
        for step in range(1, sizes[axis]):
            pl.semaphore_signal(
                barrier,
                inc=1,
                device_id={axis: lax.rem(me[axis] + step, sizes[axis])},
                device_id_type=pl.DeviceIdType.MESH,
            )
    pl.semaphore_wait(barrier, sum(sizes[axis] - 1 for axis in sizes))
    refs = list(refs)
    taken = []
    for field in (2, 3, 4):
        taken.append([])
        for job in jobs:
            taken[-1].append([refs.pop(0) for _ in range(job[field])])
    running = [
        STEPS[job[0]](job[1], sizes[job[1][0]], me[job[1][0]], *[group[i] for group in taken])
        for i, job in enumerate(jobs)
    ]
    while running:
        running = [steps for steps in running if next(steps, "over") != "over"]


def push(axis, array, src_dim, dst_dim):
    n = lax.axis_size(axis)
    block = list(array.shape)
    src_size = dst_size = None
    if src_dim == "lead":
        block = block[1:]
    elif src_dim is not None:
        block[src_dim] //= n
        src_size = block[src_dim]
    if dst_dim == "lead":
        block = [n] + block
    else:
        dst_size = block[dst_dim]
        block[dst_dim] *= n
    sems = pltpu.SemaphoreType.DMA((n - 1,))
    return (
        "push",
        (axis, src_dim, src_size, dst_dim, dst_size),
        [array],
        [jax.ShapeDtypeStruct(tuple(block), array.dtype)],
        [sems, sems, pltpu.SemaphoreType.DMA((1,))],
    )


def gather_rows(axis, array, pieces=2):
    if lax.axis_size(axis) != 4:
        return push(axis, array, None, 0)
    sems = pltpu.SemaphoreType.DMA((2 * pieces + 1,))
    return (
        "relay_gather",
        (axis, pieces),
        [array],
        [jax.ShapeDtypeStruct((4 * array.shape[0],) + array.shape[1:], array.dtype)],
        [sems, sems, pltpu.SemaphoreType.DMA((1,))],
    )


def reduce_rows(axis, array, pieces=2):
    if lax.axis_size(axis) != 4:
        return push(axis, array, 0, "lead")
    rows, width = array.shape[0] // 4, array.shape[1]
    sems = pltpu.SemaphoreType.DMA((2 * pieces + 1,))
    return (
        "relay_reduce",
        (axis, pieces),
        [array],
        [jax.ShapeDtypeStruct((rows, width), array.dtype)],
        [
            sems,
            sems,
            pltpu.VMEM((2 * rows, width), array.dtype),
            pltpu.VMEM((rows, width), array.dtype),
            pltpu.VMEM((rows, width), array.dtype),
        ],
    )


def reduce_then_gather(axis, array, base=None, gain=None, pieces=2):
    n = lax.axis_size(axis)
    rows, width = array.shape[0], array.shape[1] // n
    sems = pltpu.SemaphoreType.DMA((2 * pieces * (n - 1),))
    return (
        "reduce_gather",
        (axis, pieces, base is not None, gain is not None),
        [array] + [x for x in (base, gain) if x is not None],
        [
            jax.ShapeDtypeStruct((rows, width), jnp.float32),
            jax.ShapeDtypeStruct(array.shape, array.dtype),
        ],
        [
            sems,
            sems,
            pltpu.VMEM((n - 1, rows, width), array.dtype),
            pltpu.VMEM((rows, width), array.dtype),
        ],
    )


def exchange(ident, *jobs):
    sizes = {job[1][0]: lax.axis_size(job[1][0]) for job in jobs}
    ins = [array for job in jobs for array in job[2]]
    outs = [shape for job in jobs for shape in job[3]]
    whole = pl.BlockSpec(memory_space=pltpu.VMEM)
    return pl.pallas_call(
        functools.partial(
            exchange_kernel,
            tuple((job[0], job[1], len(job[2]), len(job[3]), len(job[4])) for job in jobs),
            sizes,
        ),
        out_shape=tuple(outs),
        in_specs=[whole] * len(ins),
        out_specs=(whole,) * len(outs),
        scratch_shapes=[scratch for job in jobs for scratch in job[4]],
        compiler_params=pltpu.CompilerParams(collective_id=ident, has_side_effects=True),
    )(*ins)


def dot(left_side, right_side):
    return jnp.dot(left_side, right_side, preferred_element_type=jnp.float32)


def dot_turned(left_side, right_side):
    return lax.dot_general(
        left_side, right_side, (((1,), (1,)), ((), ())), preferred_element_type=jnp.float32
    )


def outer_sum(left_side, right_side):
    return lax.dot_general(
        left_side, right_side, (((0,), (0,)), ((), ())), preferred_element_type=jnp.float32
    )


def eight(vector):
    return jnp.broadcast_to(vector[None, :], (8,) + vector.shape)


def added(stacked):
    return jnp.sum(stacked.astype(jnp.float32), axis=0)


def joined(reduced):
    return reduced if reduced.ndim == 2 else added(reduced).astype(reduced.dtype)


def row_rates(wide):
    return lax.rsqrt(jnp.mean(wide * wide, axis=1, keepdims=True) + epsilon)


def unfold(got):
    return jnp.moveaxis(got, 0, 1).reshape(got.shape[1], -1)


def dp_jobs(array):
    return [push("dp", array, None, "lead")] if lax.axis_size("dp") == 2 else []


def dp_total(array, got):
    return added(got[0]) if got else lax.psum(array, "dp").astype(jnp.float32)


def local(
    hidden_in,
    segments,
    norm_in,
    w_query,
    w_key,
    w_value,
    query_gain,
    key_gain,
    w_out,
    norm_mid,
    w_gate,
    w_up,
    w_down,
    cotangent,
):
    low = jnp.bfloat16
    flt = jnp.float32
    rows = lax.axis_size("row")
    slab_rows, feature_slab = hidden_in.shape
    model_width = feature_slab * rows
    q_cols = w_query.shape[1]
    k_cols = w_key.shape[1]
    q_mine = q_cols // HEAD_DIM // rows
    kv_local = k_cols // HEAD_DIM
    kv_mine = max(1, kv_local // rows)
    share = rows * kv_mine // kv_local
    groups = q_mine // kv_mine
    q_width, k_width = q_mine * HEAD_DIM, kv_mine * HEAD_DIM
    ff_local = w_gate.shape[1]
    ff_mine = ff_local // rows
    scale_factor = HEAD_DIM ** (-0.5)
    seq_local, length = segments.shape
    stream = seq_local * length
    documents = (segments + length * jnp.arange(seq_local, dtype=jnp.int32)[:, None]).reshape(
        stream
    )
    places = jnp.arange(stream, dtype=jnp.int32)
    allowed = (documents[:, None] == documents[None, :]) & (places[:, None] >= places[None, :])
    cos_table, sin_table = rotary_tables(positions_of(documents))

    cot_low = cotangent.astype(low)
    w_joined_parts = jnp.stack(
        [
            jnp.concatenate(
                [
                    w_query[:, r * q_width : (r + 1) * q_width],
                    w_key[:, (r // share) * k_width : (r // share + 1) * k_width],
                    w_value[:, (r // share) * k_width : (r // share + 1) * k_width],
                ],
                axis=1,
            )
            for r in range(rows)
        ]
    )
    w_pair_parts = jnp.stack(
        [
            jnp.stack([w[:, r * ff_mine : (r + 1) * ff_mine] for w in (w_gate, w_up)])
            for r in range(rows)
        ]
    )
    hidden_row, norm_in_all, norm_mid_all, w_joined, w_out_mine = exchange(
        0,
        push("row", hidden_in.astype(low), None, 1),
        push("row", eight(norm_in), None, 1),
        push("row", eight(norm_mid), None, 1),
        push("row", w_joined_parts, "lead", 0),
        push("row", w_out, 0, 1),
    )
    hidden_wide = hidden_row.astype(flt)
    rate_in = row_rates(hidden_wide)
    normed_in, w_pair = exchange(
        1,
        gather_rows("col", (hidden_wide * rate_in * norm_in_all[:1]).astype(low)),
        push("row", w_pair_parts, "lead", 1),
    )
    projected = dot(normed_in, w_joined)
    raw_query = projected[:, :q_width].reshape(stream, q_mine, HEAD_DIM)
    raw_key = projected[:, q_width : q_width + k_width].reshape(stream, kv_mine, HEAD_DIM)
    value_heads = projected[:, q_width + k_width :].astype(low).reshape(stream, kv_mine, HEAD_DIM)
    query_rate = head_rates(raw_query)
    key_rate = head_rates(raw_key)
    query_rot = rotate(raw_query * query_rate * query_gain, cos_table, sin_table).astype(low)
    key_heads = rotate(raw_key * key_rate * key_gain, cos_table, sin_table).astype(low)
    query_blocks = query_rot.reshape(stream, kv_mine, groups, HEAD_DIM)
    scores = (
        jnp.einsum("qkgd,skd->kgqs", query_blocks, key_heads, preferred_element_type=flt)
        * scale_factor
    )
    log_total = jnp.log(jnp.sum(jnp.where(allowed, jnp.exp(scores), 0.0), axis=-1, keepdims=True))
    probability = jnp.where(allowed, jnp.exp(scores - log_total), 0.0)
    mixed = (
        jnp.einsum(
            "kgqs,skd->qkgd", probability.astype(low), value_heads, preferred_element_type=flt
        )
        .reshape(stream, q_width)
        .astype(low)
    )
    out_cols, cot_row = exchange(
        2,
        reduce_rows("col", dot(mixed, w_out_mine).astype(low)),
        push("row", cot_low, None, 1),
    )
    cot_all = lax.all_gather(cot_row, "col", axis=0, tiled=True)
    resid, resid_row = exchange(3, reduce_then_gather("row", joined(out_cols), base=hidden_in))
    resid_wide = resid_row.astype(flt)
    rate_mid = row_rates(resid_wide)
    normed_mid, w_down_mine = exchange(
        4,
        gather_rows("col", (resid_wide * rate_mid * norm_mid_all[:1]).astype(low)),
        push("row", w_down, 0, 1),
    )
    gate_pre = dot(normed_mid, w_pair[0])
    up_pre = dot(normed_mid, w_pair[1])
    sigmoid_gate = jax.nn.sigmoid(gate_pre)
    activated = gate_pre * sigmoid_gate
    swiglu = (activated * up_pre).astype(low)
    down_part = dot(swiglu, w_down_mine).astype(low)
    down_own = lax.psum_scatter(
        lax.psum_scatter(down_part, "col", scatter_dimension=0, tiled=True),
        "row",
        scatter_dimension=1,
        tiled=True,
    )
    output = resid + down_own.astype(flt)
    grad_swiglu = dot_turned(cot_all, w_down_mine)
    grad_down = outer_sum(swiglu, cot_all).astype(low)
    grad_gate_act = (
        grad_swiglu * up_pre * sigmoid_gate * (1.0 + gate_pre * (1.0 - sigmoid_gate))
    ).astype(low)
    grad_up_act = (grad_swiglu * activated).astype(low)
    mid_part = dot_turned(grad_gate_act, w_pair[0]) + dot_turned(grad_up_act, w_pair[1])
    grad_gate = outer_sum(normed_mid, grad_gate_act).astype(low)
    grad_up = outer_sum(normed_mid, grad_up_act).astype(low)
    mid_cols, grad_down, *pair = exchange(
        5,
        reduce_rows("col", mid_part.astype(low)),
        push("row", grad_down, 1, 0),
        *dp_jobs(grad_gate),
    )
    grad_gate = dp_total(grad_gate, pair).astype(low)
    grad_normed_mid, scaled_row, *pair = exchange(
        6,
        reduce_then_gather("row", joined(mid_cols), gain=eight(norm_mid)),
        *dp_jobs(grad_up),
        *dp_jobs(grad_down),
    )
    grad_up = dp_total(grad_up, pair[:1]).astype(low)
    grad_down = dp_total(grad_down, pair[1:])
    scaled_wide = scaled_row.astype(flt)
    mid_scale = rate_mid**3 * jnp.mean(scaled_wide * resid_wide, axis=1, keepdims=True)
    grad_resid = cotangent + rate_mid * (norm_mid * grad_normed_mid) - resid * mid_scale
    gain_mid = jnp.sum(grad_normed_mid * resid * rate_mid, axis=0)
    resid_low, grad_gate_got = exchange(
        7,
        gather_rows(
            "col",
            (cot_row.astype(flt) + rate_mid * scaled_wide - resid_wide * mid_scale).astype(low),
        ),
        push("row", grad_gate, 0, "lead"),
    )
    grad_gate = unfold(grad_gate_got).astype(flt)
    grad_out = outer_sum(mixed, resid_low).astype(low)
    grad_mixed_heads = (
        dot_turned(resid_low, w_out_mine).astype(low).reshape(stream, kv_mine, groups, HEAD_DIM)
    )
    grad_value_act = jnp.einsum(
        "kgqs,qkgd->skd", probability.astype(low), grad_mixed_heads, preferred_element_type=flt
    )
    grad_probs = jnp.einsum(
        "qkgd,skd->kgqs", grad_mixed_heads, value_heads, preferred_element_type=flt
    )
    row_inner = jnp.sum(probability * grad_probs, axis=-1, keepdims=True)
    grad_scores = (probability * (grad_probs - row_inner) * scale_factor).astype(low)
    grad_query_rot = jnp.einsum(
        "kgqs,skd->qkgd", grad_scores, key_heads, preferred_element_type=flt
    ).reshape(stream, q_mine, HEAD_DIM)
    grad_key_rot = jnp.einsum(
        "kgqs,qkgd->skd", grad_scores, query_blocks, preferred_element_type=flt
    )
    grad_raw_query, gain_query = head_back(
        raw_query, query_rate, query_gain, rotate_back(grad_query_rot, cos_table, sin_table)
    )
    grad_raw_key, gain_key = head_back(
        raw_key, key_rate, key_gain, rotate_back(grad_key_rot, cos_table, sin_table)
    )
    grad_proj = jnp.concatenate(
        [
            grad_raw_query.reshape(stream, q_width),
            grad_raw_key.reshape(stream, k_width),
            grad_value_act.reshape(stream, k_width),
        ],
        axis=1,
    ).astype(low)
    grad_joined = outer_sum(normed_in, grad_proj).astype(low)
    in_part = dot_turned(grad_proj, w_joined)
    block_start = lax.axis_index("row") * feature_slab
    gain_in = jnp.sum(in_part * normed_in.astype(flt), axis=0) / norm_in_all[0]
    spread_mid = lax.dynamic_update_slice(jnp.zeros((model_width,), flt), gain_mid, (block_start,))
    gains = jnp.concatenate([gain_in, spread_mid, gain_query, gain_key])
    in_cols, grad_up_got, gains_got, *pair = exchange(
        8,
        reduce_rows("col", in_part.astype(low)),
        push("row", grad_up, 0, "lead"),
        push("dp", eight(gains), None, "lead"),
        *dp_jobs(grad_joined),
        *dp_jobs(grad_out),
    )
    in_cols = joined(in_cols)
    inner_part = jnp.sum(in_cols.astype(flt) * hidden_wide * norm_in_all[:1], axis=1)
    grad_up = unfold(grad_up_got).astype(flt)
    grad_joined = dp_total(grad_joined, pair[:1]).astype(low)
    grad_out = dp_total(grad_out, pair[1:]).astype(low)
    in_blocks, in_inner, joined_got, out_got, gains_got = exchange(
        9,
        push("row", in_cols, 1, "lead"),
        push("row", eight(inner_part), None, "lead"),
        push("row", grad_joined, 0, "lead"),
        push("row", grad_out, 1, 0),
        push("row", jnp.sum(gains_got, axis=0), None, "lead"),
    )
    (gains_got,) = exchange(10, push("col", jnp.sum(gains_got, axis=0), None, "lead"))
    gains = jnp.sum(gains_got, axis=0)[0]
    grad_normed_in = added(in_blocks)
    in_scale = rate_in**3 * (jnp.sum(in_inner, axis=0)[0][:, None] / model_width)
    grad_hidden = grad_resid + rate_in * (norm_in * grad_normed_in) - hidden_in * in_scale

    def shared(got):
        summed = got.astype(flt).reshape(rows // share, share, feature_slab, k_width).sum(axis=1)
        return unfold(summed)

    grad_query = unfold(joined_got[:, :, :q_width]).astype(flt)
    grad_key = shared(joined_got[:, :, q_width : q_width + k_width])
    grad_value = shared(joined_got[:, :, q_width + k_width :])
    grad_out = out_got.astype(flt)
    gain_in = lax.dynamic_slice(gains, (block_start,), (feature_slab,))
    gain_mid = lax.dynamic_slice(gains, (model_width + block_start,), (feature_slab,))
    gain_query = gains[2 * model_width : 2 * model_width + HEAD_DIM]
    gain_key = gains[2 * model_width + HEAD_DIM :]
    return (
        output,
        grad_hidden,
        gain_in,
        grad_query,
        grad_key,
        grad_value,
        gain_query,
        gain_key,
        grad_out,
        gain_mid,
        grad_gate,
        grad_up,
        grad_down,
    )


def solution(mesh):
    return jax.shard_map(
        local,
        mesh=mesh,
        in_specs=(
            P(("dp", "col"), "row"),
            P("dp", None),
            P("row"),
            P("row", "col"),
            P("row", "col"),
            P("row", "col"),
            P(),
            P(),
            P("col", "row"),
            P("row"),
            P("row", "col"),
            P("row", "col"),
            P("col", "row"),
            P(("dp", "col"), "row"),
        ),
        out_specs=(
            P(("dp", "col"), "row"),
            P(("dp", "col"), "row"),
            P("row"),
            P("row", "col"),
            P("row", "col"),
            P("row", "col"),
            P(),
            P(),
            P("col", "row"),
            P("row"),
            P("row", "col"),
            P("row", "col"),
            P("col", "row"),
        ),
        check_vma=False,
    )
```

```python
import functools

import jax
import jax.numpy as jnp
from jax import lax
from jax.experimental import pallas as pl
from jax.experimental.pallas import tpu as pltpu
from jax.sharding import PartitionSpec as P

HEAD_DIM = 64


epsilon = 1e-05
rope_base = 1000000.0


def positions_of(documents):
    length = documents.shape[0]
    places = jnp.arange(length, dtype=jnp.int32)
    starts_here = jnp.concatenate([places[:1] >= 0, documents[1:] != documents[:-1]])
    doc_start = lax.cummax(jnp.where(starts_here, places, 0), axis=0)
    return places - doc_start


def rotary_tables(positions):
    half_dim = HEAD_DIM // 2
    frequency = rope_base ** (-2.0 * jnp.arange(half_dim, dtype=jnp.float32) / HEAD_DIM)
    angles = positions.astype(jnp.float32)[:, None] * frequency[None, :]
    return (jnp.cos(angles)[:, None, :], jnp.sin(angles)[:, None, :])


def rotate(values, cos_table, sin_table):
    half_dim = HEAD_DIM // 2
    first_half, second = (values[..., :half_dim], values[..., half_dim:])
    return jnp.concatenate(
        [first_half * cos_table - second * sin_table, second * cos_table + first_half * sin_table],
        axis=-1,
    )


def rotate_back(gradient, cos_table, sin_table):
    half_dim = HEAD_DIM // 2
    first_half, second = (gradient[..., :half_dim], gradient[..., half_dim:])
    return jnp.concatenate(
        [first_half * cos_table + second * sin_table, second * cos_table - first_half * sin_table],
        axis=-1,
    )


def head_rates(values):
    return lax.rsqrt(jnp.mean(values * values, axis=-1, keepdims=True) + epsilon)


def head_back(values, rate_rows, gain, gradient):
    scaled = gain * gradient
    inner_mean = jnp.mean(scaled * values, axis=-1, keepdims=True)
    return (
        rate_rows * scaled - values * rate_rows**3 * inner_mean,
        jnp.sum(gradient * values * rate_rows, axis=(0, 1)),
    )


def part(ref, dim, index, size):
    if dim is None:
        return ref
    if dim == "lead":
        return ref.at[index]
    start = pl.multiple_of(index * size, size)
    return ref.at[(slice(None),) * dim + (pl.ds(start, size),)]


def send_to(src, dst, sends, recvs, slot, axis, peer):
    copy = pltpu.make_async_remote_copy(
        src_ref=src,
        dst_ref=dst,
        send_sem=sends.at[slot],
        recv_sem=recvs.at[slot],
        device_id={axis: peer},
        device_id_type=pl.DeviceIdType.MESH,
    )
    copy.start()
    return copy


def push_steps(plan, n, me, ins, outs, scratch):
    axis, src_dim, src_size, dst_dim, dst_size = plan
    sends, recvs, own = scratch
    copies = []
    for step in range(1, n):
        peer = lax.rem(me + step, n)
        copies.append(
            send_to(
                part(ins[0], src_dim, peer, src_size),
                part(outs[0], dst_dim, me, dst_size),
                sends,
                recvs,
                step - 1,
                axis,
                peer,
            )
        )
    copy = pltpu.make_async_copy(
        part(ins[0], src_dim, me, src_size), part(outs[0], dst_dim, me, dst_size), own.at[0]
    )
    copy.start()
    copies.append(copy)
    yield
    yield
    yield
    for copy in copies:
        copy.wait()


def pair_add_steps(plan, n, me, ins, outs, scratch):
    sends, recvs, got = scratch
    copy = send_to(ins[0], got, sends, recvs, 0, plan[0], lax.rem(me + 1, n))
    yield
    yield
    yield
    copy.wait()
    flt = jnp.float32
    outs[0][...] = (ins[0][...].astype(flt) + got[...].astype(flt)).astype(outs[0].dtype)


def partners(me):
    near = me + 1 - 2 * lax.rem(me, 2)
    far = lax.rem(me + 2, 4)
    return near, far, lax.rem(near + 2, 4)


def span(block, rows, piece, pieces):
    size = rows // pieces
    return pl.ds(pl.multiple_of(block * rows + piece * size, size), size)


def relay_gather_steps(plan, n, me, ins, outs, scratch):
    axis, pieces = plan
    sends, recvs, own = scratch
    rows = ins[0].shape[0]
    near, far, _ = partners(me)
    size = rows // pieces
    firsts = [
        send_to(
            ins[0].at[pl.ds(p * size, size)],
            outs[0].at[span(me, rows, p, pieces)],
            sends,
            recvs,
            p,
            axis,
            far,
        )
        for p in range(pieces)
    ]
    beside = send_to(
        ins[0], outs[0].at[span(me, rows, 0, 1)], sends, recvs, pieces, axis, near
    )
    mine = pltpu.make_async_copy(ins[0], outs[0].at[span(me, rows, 0, 1)], own.at[0])
    mine.start()
    yield
    relays = []
    for p in range(pieces):
        firsts[p].wait_recv()
        place = span(far, rows, p, pieces)
        relays.append(
            send_to(
                outs[0].at[place], outs[0].at[place], sends, recvs, pieces + 1 + p, axis, near
            )
        )
    yield
    for copy in firsts:
        copy.wait_send()
    beside.wait()
    for copy in relays:
        copy.wait()
    mine.wait()


def relay_reduce_steps(plan, n, me, ins, outs, scratch):
    axis, pieces = plan
    sends, recvs, from_near, passed, from_far = scratch
    flt = jnp.float32
    rows = outs[0].shape[0]
    size = rows // pieces
    near, far, across = partners(me)
    firsts = [
        send_to(
            ins[0].at[span(across, rows, p, pieces)],
            from_near.at[pl.ds(p * size, size)],
            sends,
            recvs,
            p,
            axis,
            near,
        )
        for p in range(pieces)
    ]
    beside = send_to(
        ins[0].at[span(near, rows, 0, 1)],
        from_near.at[pl.ds(rows, rows)],
        sends,
        recvs,
        pieces,
        axis,
        near,
    )
    yield
    seconds = []
    for p in range(pieces):
        here = pl.ds(p * size, size)
        firsts[p].wait_recv()
        passed[here, :] = (
            ins[0][span(far, rows, p, pieces), :].astype(flt) + from_near[here, :].astype(flt)
        ).astype(passed.dtype)
        seconds.append(
            send_to(
                passed.at[here], from_far.at[here], sends, recvs, pieces + 1 + p, axis, far
            )
        )
    beside.wait_recv()
    yield
    for p in range(pieces):
        here = pl.ds(p * size, size)
        seconds[p].wait_recv()
        outs[0][here, :] = (
            ins[0][span(me, rows, p, pieces), :].astype(flt)
            + from_near[pl.ds(rows + p * size, size), :].astype(flt)
            + from_far[here, :].astype(flt)
        ).astype(outs[0].dtype)
    for copy in firsts + [beside] + seconds:
        copy.wait_send()


def reduce_gather_steps(plan, n, me, ins, outs, scratch):
    axis, pieces, added_to, gained = plan
    sends, recvs, got, mine = scratch
    flt = jnp.float32
    rows, width = outs[0].shape
    size = rows // pieces
    own_columns = pl.ds(pl.multiple_of(me * width, width), width)
    arriving = []
    for p in range(pieces):
        here = pl.ds(p * size, size)
        arriving.append(
            [
                send_to(
                    ins[0].at[
                        here,
                        pl.ds(pl.multiple_of(lax.rem(me + step, n) * width, width), width),
                    ],
                    got.at[step - 1, here],
                    sends,
                    recvs,
                    p * (n - 1) + step - 1,
                    axis,
                    lax.rem(me + step, n),
                )
                for step in range(1, n)
            ]
        )
    yield
    leaving = []
    for p in range(pieces):
        here = pl.ds(p * size, size)
        total = ins[0][here, own_columns].astype(flt)
        for step in range(1, n):
            arriving[p][step - 1].wait_recv()
            total = total + got[step - 1, here].astype(flt)
        if added_to:
            total = total + ins[1][here, :]
        outs[0][here, :] = total
        if gained:
            total = total * ins[1][0:1, :]
        mine[here, :] = total.astype(mine.dtype)
        outs[1][here, own_columns] = total.astype(mine.dtype)
        for step in range(1, n):
            leaving.append(
                send_to(
                    mine.at[here],
                    outs[1].at[here, own_columns],
                    sends,
                    recvs,
                    (pieces + p) * (n - 1) + step - 1,
                    axis,
                    lax.rem(me + step, n),
                )
            )
    yield
    for copies in arriving:
        for copy in copies:
            copy.wait_send()
    for copy in leaving:
        copy.wait()


STEPS = {
    "push": push_steps,
    "pair_add": pair_add_steps,
    "relay_gather": relay_gather_steps,
    "relay_reduce": relay_reduce_steps,
    "reduce_gather": reduce_gather_steps,
}


def exchange_kernel(jobs, sizes, *refs):
    me = {axis: lax.axis_index(axis) for axis in sizes}
    barrier = pltpu.get_barrier_semaphore()
    for axis in sizes:
        for step in range(1, sizes[axis]):
            pl.semaphore_signal(
                barrier,
                inc=1,
                device_id={axis: lax.rem(me[axis] + step, sizes[axis])},
                device_id_type=pl.DeviceIdType.MESH,
            )
    pl.semaphore_wait(barrier, sum(sizes[axis] - 1 for axis in sizes))
    refs = list(refs)
    taken = []
    for field in (2, 3, 4):
        taken.append([])
        for job in jobs:
            taken[-1].append([refs.pop(0) for _ in range(job[field])])
    running = [
        STEPS[job[0]](job[1], sizes[job[1][0]], me[job[1][0]], *[group[i] for group in taken])
        for i, job in enumerate(jobs)
    ]
    while running:
        running = [steps for steps in running if next(steps, "over") != "over"]


def push(axis, array, src_dim, dst_dim):
    n = lax.axis_size(axis)
    block = list(array.shape)
    src_size = dst_size = None
    if src_dim == "lead":
        block = block[1:]
    elif src_dim is not None:
        block[src_dim] //= n
        src_size = block[src_dim]
    if dst_dim == "lead":
        block = [n] + block
    else:
        dst_size = block[dst_dim]
        block[dst_dim] *= n
    sems = pltpu.SemaphoreType.DMA((n - 1,))
    return (
        "push",
        (axis, src_dim, src_size, dst_dim, dst_size),
        [array],
        [jax.ShapeDtypeStruct(tuple(block), array.dtype)],
        [sems, sems, pltpu.SemaphoreType.DMA((1,))],
    )


def gather_rows(axis, array, pieces=4):
    if lax.axis_size(axis) != 4:
        return push(axis, array, None, 0)
    sems = pltpu.SemaphoreType.DMA((2 * pieces + 1,))
    return (
        "relay_gather",
        (axis, pieces),
        [array],
        [jax.ShapeDtypeStruct((4 * array.shape[0],) + array.shape[1:], array.dtype)],
        [sems, sems, pltpu.SemaphoreType.DMA((1,))],
    )


def reduce_rows(axis, array, pieces=4):
    if lax.axis_size(axis) != 4:
        return push(axis, array, 0, "lead")
    rows, width = array.shape[0] // 4, array.shape[1]
    sems = pltpu.SemaphoreType.DMA((2 * pieces + 1,))
    return (
        "relay_reduce",
        (axis, pieces),
        [array],
        [jax.ShapeDtypeStruct((rows, width), array.dtype)],
        [
            sems,
            sems,
            pltpu.VMEM((2 * rows, width), array.dtype),
            pltpu.VMEM((rows, width), array.dtype),
            pltpu.VMEM((rows, width), array.dtype),
        ],
    )


def reduce_then_gather(axis, array, base=None, gain=None, pieces=2):
    n = lax.axis_size(axis)
    rows, width = array.shape[0], array.shape[1] // n
    sems = pltpu.SemaphoreType.DMA((2 * pieces * (n - 1),))
    return (
        "reduce_gather",
        (axis, pieces, base is not None, gain is not None),
        [array] + [x for x in (base, gain) if x is not None],
        [
            jax.ShapeDtypeStruct((rows, width), jnp.float32),
            jax.ShapeDtypeStruct(array.shape, array.dtype),
        ],
        [
            sems,
            sems,
            pltpu.VMEM((n - 1, rows, width), array.dtype),
            pltpu.VMEM((rows, width), array.dtype),
        ],
    )


def exchange(ident, *jobs):
    sizes = {job[1][0]: lax.axis_size(job[1][0]) for job in jobs}
    ins = [array for job in jobs for array in job[2]]
    outs = [shape for job in jobs for shape in job[3]]
    whole = pl.BlockSpec(memory_space=pltpu.VMEM)
    return pl.pallas_call(
        functools.partial(
            exchange_kernel,
            tuple((job[0], job[1], len(job[2]), len(job[3]), len(job[4])) for job in jobs),
            sizes,
        ),
        out_shape=tuple(outs),
        in_specs=[whole] * len(ins),
        out_specs=(whole,) * len(outs),
        scratch_shapes=[scratch for job in jobs for scratch in job[4]],
        compiler_params=pltpu.CompilerParams(collective_id=ident, has_side_effects=True),
    )(*ins)


def dot(left_side, right_side):
    return jnp.dot(left_side, right_side, preferred_element_type=jnp.float32)


def dot_turned(left_side, right_side):
    return lax.dot_general(
        left_side, right_side, (((1,), (1,)), ((), ())), preferred_element_type=jnp.float32
    )


def outer_sum(left_side, right_side):
    return lax.dot_general(
        left_side, right_side, (((0,), (0,)), ((), ())), preferred_element_type=jnp.float32
    )


def eight(vector):
    return jnp.broadcast_to(vector[None, :], (8,) + vector.shape)


def added(stacked):
    return jnp.sum(stacked.astype(jnp.float32), axis=0)


def joined(reduced):
    return reduced if reduced.ndim == 2 else added(reduced).astype(reduced.dtype)


def row_rates(wide):
    return lax.rsqrt(jnp.mean(wide * wide, axis=1, keepdims=True) + epsilon)


def dp_jobs(array):
    if lax.axis_size("dp") != 2:
        return []
    sems = pltpu.SemaphoreType.DMA((1,))
    return [
        (
            "pair_add",
            ("dp",),
            [array],
            [jax.ShapeDtypeStruct(array.shape, array.dtype)],
            [sems, sems, pltpu.VMEM(array.shape, array.dtype)],
        )
    ]


def dp_total(array, got):
    return got[0] if got else lax.psum(array, "dp")


def local(
    hidden_in,
    segments,
    norm_in,
    w_query,
    w_key,
    w_value,
    query_gain,
    key_gain,
    w_out,
    norm_mid,
    w_gate,
    w_up,
    w_down,
    cotangent,
):
    low = jnp.bfloat16
    flt = jnp.float32
    rows = lax.axis_size("row")
    slab_rows, feature_slab = hidden_in.shape
    model_width = feature_slab * rows
    q_cols = w_query.shape[1]
    k_cols = w_key.shape[1]
    q_mine = q_cols // HEAD_DIM // rows
    kv_local = k_cols // HEAD_DIM
    kv_mine = max(1, kv_local // rows)
    share = rows * kv_mine // kv_local
    groups = q_mine // kv_mine
    q_width, k_width = q_mine * HEAD_DIM, kv_mine * HEAD_DIM
    scale_factor = HEAD_DIM ** (-0.5)
    seq_local, length = segments.shape
    stream = seq_local * length
    documents = (segments + length * jnp.arange(seq_local, dtype=jnp.int32)[:, None]).reshape(
        stream
    )
    places = jnp.arange(stream, dtype=jnp.int32)
    allowed = (documents[:, None] == documents[None, :]) & (places[:, None] >= places[None, :])
    cos_table, sin_table = rotary_tables(positions_of(documents))

    cot_low = cotangent.astype(low)
    query_turned, key_turned, value_turned = w_query.T, w_key.T, w_value.T
    w_joined_parts = jnp.stack(
        [
            jnp.concatenate(
                [
                    query_turned[r * q_width : (r + 1) * q_width],
                    key_turned[(r // share) * k_width : (r // share + 1) * k_width],
                    value_turned[(r // share) * k_width : (r // share + 1) * k_width],
                ],
                axis=0,
            )
            for r in range(rows)
        ]
    )
    hidden_row, norm_in_all, norm_mid_all, w_joined, w_out_mine = exchange(
        0,
        push("row", hidden_in.astype(low), None, 1),
        push("row", eight(norm_in), None, 1),
        push("row", eight(norm_mid), None, 1),
        push("row", w_joined_parts, "lead", 1),
        push("row", w_out, 0, 1),
    )
    hidden_wide = hidden_row.astype(flt)
    rate_in = row_rates(hidden_wide)
    normed_in, w_gate_mine, w_up_mine = exchange(
        1,
        gather_rows("col", (hidden_wide * rate_in * norm_in_all[:1]).astype(low)),
        push("row", w_gate.T, 0, 1),
        push("row", w_up.T, 0, 1),
    )
    projected = dot_turned(normed_in, w_joined)
    raw_query = projected[:, :q_width].reshape(stream, q_mine, HEAD_DIM)
    raw_key = projected[:, q_width : q_width + k_width].reshape(stream, kv_mine, HEAD_DIM)
    value_heads = projected[:, q_width + k_width :].astype(low).reshape(stream, kv_mine, HEAD_DIM)
    query_rate = head_rates(raw_query)
    key_rate = head_rates(raw_key)
    query_rot = rotate(raw_query * query_rate * query_gain, cos_table, sin_table).astype(low)
    key_heads = rotate(raw_key * key_rate * key_gain, cos_table, sin_table).astype(low)
    query_blocks = query_rot.reshape(stream, kv_mine, groups, HEAD_DIM)
    scores = (
        jnp.einsum("qkgd,skd->kgqs", query_blocks, key_heads, preferred_element_type=flt)
        * scale_factor
    )
    log_total = jnp.log(jnp.sum(jnp.where(allowed, jnp.exp(scores), 0.0), axis=-1, keepdims=True))
    probability = jnp.where(allowed, jnp.exp(scores - log_total), 0.0)
    mixed = (
        jnp.einsum(
            "kgqs,skd->qkgd", probability.astype(low), value_heads, preferred_element_type=flt
        )
        .reshape(stream, q_width)
        .astype(low)
    )
    out_cols, cot_row = exchange(
        2,
        reduce_rows("col", dot(mixed, w_out_mine).astype(low)),
        push("row", cot_low, None, 1),
    )
    cot_all = lax.all_gather(cot_row, "col", axis=0, tiled=True)
    resid, resid_row = exchange(3, reduce_then_gather("row", joined(out_cols), base=hidden_in))
    resid_wide = resid_row.astype(flt)
    rate_mid = row_rates(resid_wide)
    normed_mid, w_down_mine = exchange(
        4,
        gather_rows("col", (resid_wide * rate_mid * norm_mid_all[:1]).astype(low)),
        push("row", w_down, 0, 1),
    )
    gate_pre = dot_turned(normed_mid, w_gate_mine)
    up_pre = dot_turned(normed_mid, w_up_mine)
    sigmoid_gate = jax.nn.sigmoid(gate_pre)
    activated = gate_pre * sigmoid_gate
    swiglu = (activated * up_pre).astype(low)
    down_part = dot(swiglu, w_down_mine).astype(low)
    grad_swiglu = dot_turned(cot_all, w_down_mine)
    grad_down = outer_sum(swiglu, cot_all).astype(low)
    grad_gate_act = (
        grad_swiglu * up_pre * sigmoid_gate * (1.0 + gate_pre * (1.0 - sigmoid_gate))
    ).astype(low)
    grad_up_act = (grad_swiglu * activated).astype(low)
    mid_part = dot(grad_gate_act, w_gate_mine) + dot(grad_up_act, w_up_mine)
    grad_gate = outer_sum(grad_gate_act, normed_mid).astype(low)
    grad_up = outer_sum(grad_up_act, normed_mid).astype(low)
    mid_cols, grad_down, *pair = exchange(
        5,
        reduce_rows("col", mid_part.astype(low)),
        push("row", grad_down, 1, 0),
        *dp_jobs(grad_gate),
    )
    grad_gate = dp_total(grad_gate, pair)
    grad_normed_mid, scaled_row, down_cols, *pair = exchange(
        6,
        reduce_then_gather("row", joined(mid_cols), gain=eight(norm_mid)),
        reduce_rows("col", down_part),
        *dp_jobs(grad_up),
        *dp_jobs(grad_down),
    )
    grad_up = dp_total(grad_up, pair[:1])
    grad_down = dp_total(grad_down, pair[1:]).astype(flt)
    scaled_wide = scaled_row.astype(flt)
    mid_scale = rate_mid**3 * jnp.mean(scaled_wide * resid_wide, axis=1, keepdims=True)
    grad_resid = cotangent + rate_mid * (norm_mid * grad_normed_mid) - resid * mid_scale
    gain_mid = jnp.sum(grad_normed_mid * resid * rate_mid, axis=0)
    resid_low, grad_gate, down_blocks = exchange(
        7,
        gather_rows(
            "col",
            (cot_row.astype(flt) + rate_mid * scaled_wide - resid_wide * mid_scale).astype(low),
        ),
        push("row", grad_gate, 1, 0),
        push("row", joined(down_cols), 1, "lead"),
    )
    grad_gate = grad_gate.T.astype(flt)
    output = resid + added(down_blocks)
    grad_out = outer_sum(mixed, resid_low).astype(low)
    grad_mixed_heads = (
        dot_turned(resid_low, w_out_mine).astype(low).reshape(stream, kv_mine, groups, HEAD_DIM)
    )
    grad_value_act = jnp.einsum(
        "kgqs,qkgd->skd", probability.astype(low), grad_mixed_heads, preferred_element_type=flt
    )
    grad_probs = jnp.einsum(
        "qkgd,skd->kgqs", grad_mixed_heads, value_heads, preferred_element_type=flt
    )
    row_inner = jnp.sum(probability * grad_probs, axis=-1, keepdims=True)
    grad_scores = (probability * (grad_probs - row_inner) * scale_factor).astype(low)
    grad_query_rot = jnp.einsum(
        "kgqs,skd->qkgd", grad_scores, key_heads, preferred_element_type=flt
    ).reshape(stream, q_mine, HEAD_DIM)
    grad_key_rot = jnp.einsum(
        "kgqs,qkgd->skd", grad_scores, query_blocks, preferred_element_type=flt
    )
    grad_raw_query, gain_query = head_back(
        raw_query, query_rate, query_gain, rotate_back(grad_query_rot, cos_table, sin_table)
    )
    grad_raw_key, gain_key = head_back(
        raw_key, key_rate, key_gain, rotate_back(grad_key_rot, cos_table, sin_table)
    )
    grad_proj = jnp.concatenate(
        [
            grad_raw_query.reshape(stream, q_width),
            grad_raw_key.reshape(stream, k_width),
            grad_value_act.reshape(stream, k_width),
        ],
        axis=1,
    ).astype(low)
    grad_joined = outer_sum(grad_proj, normed_in).astype(low)
    in_part = dot(grad_proj, w_joined)
    block_start = lax.axis_index("row") * feature_slab
    gain_in = jnp.sum(in_part * normed_in.astype(flt), axis=0) / norm_in_all[0]
    spread_mid = lax.dynamic_update_slice(jnp.zeros((model_width,), flt), gain_mid, (block_start,))
    gains = jnp.concatenate([gain_in, spread_mid, gain_query, gain_key])
    in_cols, grad_up, gains_got, *pair = exchange(
        8,
        reduce_rows("col", in_part.astype(low)),
        push("row", grad_up, 1, 0),
        push("dp", eight(gains), None, "lead"),
        *dp_jobs(grad_joined),
        *dp_jobs(grad_out),
    )
    in_cols = joined(in_cols)
    inner_part = jnp.sum(in_cols.astype(flt) * hidden_wide * norm_in_all[:1], axis=1)
    grad_up = grad_up.T.astype(flt)
    grad_joined = dp_total(grad_joined, pair[:1])
    grad_out = dp_total(grad_out, pair[1:])
    in_blocks, in_inner, joined_got, out_got, gains_got = exchange(
        9,
        push("row", in_cols, 1, "lead"),
        push("row", eight(inner_part), None, "lead"),
        push("row", grad_joined, 1, "lead"),
        push("row", grad_out, 1, 0),
        push("row", jnp.sum(gains_got, axis=0), None, "lead"),
    )
    (gains_got,) = exchange(10, push("col", jnp.sum(gains_got, axis=0), None, "lead"))
    gains = jnp.sum(gains_got, axis=0)[0]
    grad_normed_in = added(in_blocks)
    in_scale = rate_in**3 * (jnp.sum(in_inner, axis=0)[0][:, None] / model_width)
    grad_hidden = grad_resid + rate_in * (norm_in * grad_normed_in) - hidden_in * in_scale

    def shared(got):
        summed = got.astype(flt).reshape(rows // share, share, k_width, feature_slab).sum(axis=1)
        return summed.reshape(k_cols, feature_slab).T

    grad_query = joined_got[:, :q_width].reshape(q_cols, feature_slab).T.astype(flt)
    grad_key = shared(joined_got[:, q_width : q_width + k_width])
    grad_value = shared(joined_got[:, q_width + k_width :])
    grad_out = out_got.astype(flt)
    gain_in = lax.dynamic_slice(gains, (block_start,), (feature_slab,))
    gain_mid = lax.dynamic_slice(gains, (model_width + block_start,), (feature_slab,))
    gain_query = gains[2 * model_width : 2 * model_width + HEAD_DIM]
    gain_key = gains[2 * model_width + HEAD_DIM :]
    return (
        output,
        grad_hidden,
        gain_in,
        grad_query,
        grad_key,
        grad_value,
        gain_query,
        gain_key,
        grad_out,
        gain_mid,
        grad_gate,
        grad_up,
        grad_down,
    )


def solution(mesh):
    return jax.shard_map(
        local,
        mesh=mesh,
        in_specs=(
            P(("dp", "col"), "row"),
            P("dp", None),
            P("row"),
            P("row", "col"),
            P("row", "col"),
            P("row", "col"),
            P(),
            P(),
            P("col", "row"),
            P("row"),
            P("row", "col"),
            P("row", "col"),
            P("col", "row"),
            P(("dp", "col"), "row"),
        ),
        out_specs=(
            P(("dp", "col"), "row"),
            P(("dp", "col"), "row"),
            P("row"),
            P("row", "col"),
            P("row", "col"),
            P("row", "col"),
            P(),
            P(),
            P("col", "row"),
            P("row"),
            P("row", "col"),
            P("row", "col"),
            P("col", "row"),
        ),
        check_vma=False,
    )
```
